768 devices in a mesh: dp: 8 (over y_hi, x), zero: 96 (over z, y_lo, core).
Axes of the slice: x: 4, y: 8 (y_hi: 2, y_lo: 4; y = y_hi * 4 + y_lo), z: 12, core: 2. Of those that a mesh axis runs over, the one named last changes fastest.
Arguments:
- feats: bfloat16 [98304, 6144], P(('dp', 'zero')), may hold values from -6 to 6
- short_filter: bfloat16 [7, 6144], P(None, 'zero'), may hold values from -2 to 2
- medium_filter: float32 [128, 128], replicated, may hold values from -0.5 to 0.5
- doc_ids: int32 [768, 128], P(('dp', 'zero')), may hold values from 0 to 2, never falling along the last dimension, each value on 1 to 112 neighbouring positions
- counts: int32 [768], P(('dp', 'zero')), may hold values from 64 to 128
- plan: int32 [768], P(('dp', 'zero')), may hold values from 0 to 7, as said below
- cotangent: bfloat16 [98304, 2048], P(('dp', 'zero')), may hold values from -6 to 6
Outputs:
- mixed: bfloat16 [98304, 2048], P(('dp', 'zero'))
- feats_grad: bfloat16 [98304, 6144], P(('dp', 'zero'))
- short_grad: float32 [7, 6144], P(None, 'zero')
- medium_grad: float32 [128, 128], replicated
The draws below stay inside these ranges and needn't reach their ends.
Inputs may be any that keep to these rules, and one draw needn't show every extreme that they name: `plan`: every data rank is named by some tile.
All inputs are finite; a program needn't handle non-finite values.
Results may differ from the reference program's by a relative error of at most 0.0058.
Values may be sent and summed in bfloat16 or wider, within the bound.
No kernel may reach another device: no remote copies, remote signals or barrier semaphores. Data moves between devices by JAX's collectives and lax.ppermute only.
A program may use at most 64 MiB of HBM per device.

```python
import math
import jax
import jax.numpy as jnp
import numpy as np
from jax import lax

GROUPS = 128
SHORT = 7
MED = 128
TILE = 128
CH = 2048
TILES = 768
TOKENS = 98304
RANKS = 8
N_DP = 8


def draw_plan(key, part):
    draw_one, draw_two = jax.random.split(key)
    first_pick = jax.random.randint(draw_one, (TILES,), 0, RANKS)
    second_pick = jax.random.randint(draw_two, (TILES,), 0, RANKS)
    chosen = jnp.minimum(first_pick, second_pick)
    return chosen.at[:RANKS].set(jnp.arange(RANKS, dtype=jnp.int32)).astype(jnp.int32)


def set_ends(array, stream_key, least, top_value):
    shape = array.shape
    index_at = [jax.random.randint(jax.random.fold_in(stream_key, axis), (), 0, shape[axis]) for axis in range(len(shape))]
    array = array.at[tuple(index_at)].set(least)
    longest = shape.index(max(shape))
    index_at[longest] = (index_at[longest] + 1) % shape[longest]
    return array.at[tuple(index_at)].set(top_value)


def shard_levels(rng, dims, shards, smallest, top_value):
    level, own = 1.0, jax.random.fold_in(rng, 6)
    for dim, parts in shards:
        steps = jnp.exp(jax.random.uniform(jax.random.fold_in(own, dim), (parts,), jnp.float32, smallest / len(shards), top_value / len(shards)))
        level = level * jnp.repeat(steps, dims[dim] // parts).reshape([-1 if axis == dim else 1 for axis in range(len(dims))])
    return level


def profile(amount, total, bound, lean):
    portions = [(1 << 20) // math.isqrt(standing ** lean) + 1 for standing in range(2, amount + 1)]
    spare, given = total - bound - (amount - 1), [1] * (amount - 1)
    while spare > 0:
        free = [i for i in range(amount - 1) if given[i] < bound]
        pool, budget = sum([portions[i] for i in free]), spare
        for i in free:
            addition = min(bound - given[i], max(1, budget * portions[i] // pool), spare)
            given[i] = given[i] + addition
            spare = spare - addition
    return np.array([bound] + given)


def ragged(rng, number_of, total, reach, lean):
    if number_of == 2:
        one = jax.random.randint(rng, (), max(1, total - reach), min(reach, total - 1) + 1)
        return jnp.stack([one, total - one])
    sizes = jnp.asarray(profile(number_of, total, reach, lean), jnp.int32)
    couples = (number_of - 1) // 2
    donor, taker = sizes[1:1 + 2 * couples:2], sizes[2:2 + 2 * couples:2]
    slack = jnp.minimum(donor - 1, reach - taker)
    passed = jax.random.randint(jax.random.fold_in(rng, 1), (couples,), 0, 1 << 20) % (slack + 1)
    sizes = sizes.at[1:1 + 2 * couples:2].set(donor - passed).at[2:2 + 2 * couples:2].set(taker + passed)
    return sizes[jax.random.permutation(jax.random.fold_in(rng, 2), number_of)]


def scatter_about(own_key, dims, spread, reach, shards=(), held_as=jnp.bfloat16):
    entries = spread * jax.random.normal(own_key, dims, jnp.float32)
    if shards:
        entries = entries * shard_levels(own_key, dims, shards, -0.22, 0.18)
    return jnp.clip(entries, -reach, reach).astype(held_as)


def setup_inputs(seed: int = 0) -> dict:
    arg_keys = jax.random.split(jax.random.key(seed), 8)
    feats = scatter_about(arg_keys[0], (TOKENS, 3 * CH), 1.0, 6.0, ((0, 768),))
    short_filter = scatter_about(arg_keys[1], (SHORT, 3 * CH), SHORT ** -0.5, 2.0, ((1, 96),))
    medium_filter = scatter_about(arg_keys[2], (MED, GROUPS), MED ** -0.5, 0.5, (), jnp.float32)
    doc_ids = jax.vmap(lambda own: jnp.searchsorted(jnp.cumsum(ragged(own, 3, TILE, TILE - TILE // 8, 0)), jnp.arange(TILE), side="right"))(jax.random.split(arg_keys[3], TILES)).reshape((TILES, TILE)).astype(jnp.int32)
    counts = set_ends(jax.random.randint(arg_keys[4], (TILES,), TILE // 2, TILE + 1), jax.random.fold_in(arg_keys[4], 1), TILE // 2, TILE).astype(jnp.int32)
    plan = draw_plan(jax.random.fold_in(arg_keys[7], 71), 0)
    cotangent = scatter_about(arg_keys[6], (TOKENS, CH), 1.0, 6.0, ((0, 768),))
    return dict(feats=feats, short_filter=short_filter, medium_filter=medium_filter, doc_ids=doc_ids, counts=counts, plan=plan, cotangent=cotangent)


def toeplitz_blocks(filters):
    groups, length = filters.shape
    padded = jnp.concatenate([filters[:, ::-1], jnp.zeros((groups, length), filters.dtype)], 1)
    repeated = jnp.broadcast_to(padded[:, None, :], (groups, length, 2 * length))
    flattened = repeated.reshape(groups, 2 * length * length)[:, : length * (2 * length - 1)]
    return flattened.reshape(groups, length, 2 * length - 1)[:, :, length - 1:]


def diagonal_sums(crossed):
    groups, length, _ = crossed.shape
    padded = jnp.concatenate([crossed[:, :, ::-1], jnp.zeros_like(crossed)], 2)
    flattened = padded.reshape(groups, 2 * length * length)[:, : length * (2 * length - 1)]
    skewed = flattened.reshape(groups, length, 2 * length - 1)[:, :, length - 1:]
    return jnp.sum(skewed, 1)


def shift_down(values, offset):
    return jnp.concatenate([jnp.zeros((offset, values.shape[1]), values.dtype), values[: values.shape[0] - offset]], 0)


def shift_up(values, offset):
    return jnp.concatenate([values[offset:], jnp.zeros((offset, values.shape[1]), values.dtype)], 0)


def short_masks(segment, length):
    masks = []
    for offset in range(SHORT):
        earlier = jnp.concatenate([jnp.full((offset,), -1, jnp.int32), segment[: length - offset]])
        masks.append((earlier == segment).astype(jnp.float32)[:, None])
    return masks


def tile_terms(inputs, blocks, filters, width):
    feats, segment, count, weighting, cotangent = inputs
    length = feats.shape[0]
    groups = blocks.shape[0]
    masks = short_masks(segment, length)
    position = jnp.arange(length)
    living = (position < count).astype(jnp.float32)[:, None]
    convolved = jnp.zeros(feats.shape, jnp.float32)
    for offset in range(SHORT):
        convolved = convolved + filters[offset] * shift_down(feats, offset).astype(jnp.float32) * masks[offset]
    query_part = convolved[:, :width]
    key_part = convolved[:, width:2 * width]
    value_part = convolved[:, 2 * width:]
    product = (key_part * value_part).astype(jnp.bfloat16)
    product_groups = product.reshape(length, groups, width // groups).astype(jnp.float32)
    same_doc = (segment[:, None] == segment[None, :]) & (position[:, None] >= position[None, :])
    toeplitz = jnp.where(same_doc[None], blocks, jnp.zeros_like(blocks)).astype(jnp.float32)
    long_conv = jnp.einsum("gts,sgc->tgc", toeplitz, product_groups).reshape(length, width)
    mixed = (living * query_part * long_conv).astype(jnp.bfloat16)
    grad_out = cotangent.astype(jnp.float32) * living * weighting
    grad_query = grad_out * long_conv
    grad_long = (grad_out * query_part).astype(jnp.bfloat16)
    grad_groups = grad_long.reshape(length, groups, width // groups).astype(jnp.float32)
    grad_product = jnp.einsum("gts,tgc->sgc", toeplitz, grad_groups).reshape(length, width)
    crossed = jnp.einsum("tgc,sgc->gts", grad_groups, product_groups)
    crossed = jnp.where(same_doc[None], crossed, jnp.zeros_like(crossed))
    medium_part = diagonal_sums(crossed)
    grad_short = jnp.concatenate([grad_query, grad_product * value_part, grad_product * key_part], 1)
    grad_feats = jnp.zeros(feats.shape, jnp.float32)
    short_rows = []
    for offset in range(SHORT):
        masked = grad_short * masks[offset]
        grad_feats = grad_feats + filters[offset] * shift_up(masked, offset)
        short_rows.append(jnp.sum(masked * shift_down(feats, offset).astype(jnp.float32), 0))
    return mixed, grad_feats.astype(jnp.bfloat16), jnp.stack(short_rows), medium_part


def reference(feats, short_filter, medium_filter, doc_ids, counts, plan, cotangent):
    tile_count = counts.shape[0]
    width = cotangent.shape[1]
    member = (plan[:, None] == jnp.arange(N_DP)[None, :]).astype(jnp.float32)
    totals = jnp.sum(member * counts.astype(jnp.float32)[:, None], 0)
    weighting = TILE * tile_count / (N_DP * jnp.sum(member * totals[None, :], 1))
    blocks = toeplitz_blocks(medium_filter.astype(jnp.bfloat16).T)
    filters = short_filter.astype(jnp.float32)

    def per_tile(inputs):
        return tile_terms(inputs, blocks, filters, width)

    results = lax.map(per_tile, (feats.reshape(tile_count, TILE, 3 * width), doc_ids, counts, weighting,
                                 cotangent.reshape(tile_count, TILE, width)))
    mixed = results[0].reshape(tile_count * TILE, width)
    feats_grad = results[1].reshape(tile_count * TILE, 3 * width)
    return mixed, feats_grad, jnp.sum(results[2], 0), jnp.sum(results[3], 0).T
```

```python
import jax
import jax.numpy as jnp
from jax import lax
from jax.experimental import pallas as pl
from jax.experimental.pallas import tpu as pltpu
from jax.sharding import Mesh, PartitionSpec as P

SHORT = 7
TILE = 128
LANES = 128
WIDTH = 256
GSIZE = 16
SUB = 8
F32, BF16 = jnp.float32, jnp.bfloat16

PARTS = (("y_hi", 2), ("x", 4), ("z", 12), ("y_lo", 4), ("core", 2))
Y = ("y_hi", "y_lo", "core")
XZ = ("x", "z")
ALL = tuple(name for name, _ in PARTS)
ZERO = ("z", "y_lo", "core")
N_Y = 16
N_Z = 12
N_YL = 4


def iota(shape, dim):
    return lax.broadcasted_iota(jnp.int32, shape, dim)


def exchange(values, axes):
    return lax.all_to_all(values, axes, 0, 0, tiled=True)


def pair_kernel(x_ref, got_ref, out_ref):
    lane = iota((SUB, LANES), 1)
    row = iota((SUB, LANES), 0)
    tiles = [got_ref[i].astype(F32) for i in range(N_Y)]
    live = tiles[0]
    for tile in tiles[1:]:
        live = live + tile
    high = jnp.floor(live * (1.0 / 64.0))
    low = pltpu.roll(live - 64.0 * high, SUB, 1)
    live = jnp.where(lane < SUB, high, jnp.where(lane < 2 * SUB, low, 0.0))
    out = jnp.zeros((SUB, LANES), F32)
    for yl in range(N_YL):
        both = jnp.where(lane < 64, tiles[2 * yl], pltpu.roll(tiles[2 * yl + 1], 64, 1))
        out = jnp.where(x_ref[0] == yl, both, out)
    out = jnp.where(row == SHORT, live, out).astype(BF16)
    for i in range(out_ref.shape[0]):
        out_ref[i] = out


def merge_kernel(got_ref, out_ref):
    total = got_ref[0].astype(F32)
    for i in range(1, N_Y):
        total = total + got_ref[i].astype(F32)
    medium = total[4 * N_Z :]
    for z in range(N_Z):
        tile = jnp.concatenate([total[4 * z : 4 * z + 4], medium, jnp.zeros((4, LANES), F32)], 0).astype(BF16)
        for x in range(out_ref.shape[0] // N_Z):
            out_ref[x * N_Z + z] = tile


def final_kernel(got_ref, short_ref, out_ref):
    total = got_ref[0].astype(F32)
    for i in range(1, got_ref.shape[0]):
        total = total + got_ref[i].astype(F32)
    short_ref[0:4, :] = total[0:4, :64]
    short_ref[4:SHORT, :] = total[0 : SHORT - 4, 64:]
    medium = total[4:12].astype(BF16)
    for i in range(out_ref.shape[0]):
        out_ref[i] = medium


def tile_kernel(
    count_ref, plan_ref, seg_ref, fq_ref, fk_ref, fv_ref, sq_ref, sk_ref, sv_ref,
    every_ref, medium_ref, cot_ref,
    mixed_ref, dfeats_ref, msg_ref,
    down_ref, up_ref, lower_ref, upper_ref, flip_ref, linked_ref, scale_ref,
    taps_ref, rtaps_ref, short_ref, med_ref, stage_ref, sems,
):
    rows, cols = iota((TILE, TILE), 0), iota((TILE, TILE), 1)
    step, steps = pl.program_id(0), pl.num_programs(0)
    halves = WIDTH // LANES
    per_half = LANES // GSIZE

    @pl.when(step == 0)
    def _():
        along = jnp.broadcast_to(seg_ref[...].astype(F32), (TILE, TILE))
        same = along == along.T
        lower_ref[...] = jnp.where(same & (rows >= cols), 1.0, 0.0)
        upper = jnp.where(same & (rows <= cols), 1.0, 0.0)
        upper_ref[...] = upper
        for j in range(1, SHORT):
            down_ref[pl.ds((j - 1) * TILE, TILE), :] = jnp.where(same & (rows - cols == j), 1.0, 0.0).astype(BF16)
            up_ref[:, pl.ds((j - 1) * TILE, TILE)] = jnp.where(same & (cols - rows == j), 1.0, 0.0).astype(BF16)
        flip = jnp.where(rows + cols == TILE - 1, 1.0, 0.0).astype(BF16)
        flip_ref[...] = flip
        linked_ref[...] = jnp.dot(flip, upper.astype(BF16), preferred_element_type=F32)
        taps = medium_ref[...].T.astype(BF16)
        taps_ref[...] = taps.astype(F32)
        rtaps_ref[...] = pltpu.roll(jnp.dot(taps, flip, preferred_element_type=F32), 1, 1)
        live = every_ref[0].astype(F32)
        for i in range(1, every_ref.shape[0]):
            live = live + every_ref[i].astype(F32)
        row8, lane8 = iota((SUB, LANES), 0), iota((SUB, LANES), 1)
        high = jnp.where((row8 == SHORT) & (lane8 == plan_ref[0]), 64.0 * live, 0.0)
        low = jnp.where((row8 == SHORT) & (lane8 == plan_ref[0] + SUB), live, 0.0)
        total = jnp.sum(jnp.sum(high + low, 0, keepdims=True), 1, keepdims=True)
        tiles = every_ref.shape[0] * N_Y
        weighting = (TILE * tiles / SUB) / jnp.broadcast_to(total, (TILE, TILE))
        scale_ref[...] = jnp.where(rows < count_ref[0], weighting, 0.0)

    slot = lax.rem(step, 2)

    def store(part, at):
        where = pl.multiple_of((part * steps + at) * WIDTH, WIDTH)
        return pltpu.make_async_copy(
            stage_ref.at[lax.rem(at, 2), part], dfeats_ref.at[:, pl.ds(where, WIDTH)],
            sems.at[lax.rem(at, 2), part],
        )

    lower = lower_ref[...] > 0.5
    upper = upper_ref[...] > 0.5
    linked = linked_ref[...] > 0.5
    scale = jnp.concatenate([scale_ref[...]] * halves, 1)
    living = iota((TILE, WIDTH), 0) < count_ref[0]
    lane_group = iota((TILE, LANES), 1) // GSIZE

    def conv(f_ref, s_ref):
        feats = f_ref[...]
        taps = jnp.concatenate([s_ref[h, 0].astype(F32) for h in range(halves)], 1)
        shifted = jnp.dot(down_ref[...], feats, preferred_element_type=F32)
        total = feats.astype(F32) * taps[0:1]
        for j in range(1, SHORT):
            total = total + shifted[(j - 1) * TILE : j * TILE] * taps[j : j + 1]
        return total, shifted, taps

    query, q_shift, q_taps = conv(fq_ref, sq_ref)
    key, k_shift, k_taps = conv(fk_ref, sk_ref)
    value, v_shift, v_taps = conv(fv_ref, sv_ref)
    product = (key * value).astype(BF16)
    flipped = jnp.dot(flip_ref[...], product, preferred_element_type=F32).astype(BF16)
    gout = cot_ref[...].astype(F32) * scale
    glong = (gout * query).astype(BF16)
    zero = jnp.zeros((TILE, LANES), BF16)
    taps_here = taps_ref[pl.ds(pl.multiple_of(step * halves * per_half, halves * per_half), halves * per_half), :]
    rtaps_here = rtaps_ref[pl.ds(pl.multiple_of(step * halves * per_half, halves * per_half), halves * per_half), :]

    longs, gprods = [], []
    for half in range(halves):
        lanes = slice(half * LANES, (half + 1) * LANES)
        prod_half, glong_half, flip_half = product[:, lanes], glong[:, lanes], flipped[:, lanes]
        forward, backward, prods, glongs, flips = [], [], [], [], []
        for g in range(per_half):
            row = half * per_half + g
            base = jnp.broadcast_to(rtaps_here[row : row + 1, :], (TILE, TILE))
            forward.append(
                jnp.where(lower, pltpu.roll(base, 0, 1, stride=1, stride_axis=0), 0.0).astype(BF16)
            )
            base = jnp.broadcast_to(taps_here[row : row + 1, :], (TILE, TILE))
            backward.append(
                jnp.where(upper, pltpu.roll(base, 0, 1, stride=1, stride_axis=0), 0.0).astype(BF16)
            )
            prods.append(jnp.where(lane_group == g, prod_half, zero))
            glongs.append(jnp.where(lane_group == g, glong_half, zero))
            flips.append(jnp.where(lane_group == g, flip_half, zero))
        longs.append(
            jnp.dot(jnp.concatenate(forward, 1), jnp.concatenate(prods, 0), preferred_element_type=F32)
        )
        gprods.append(
            jnp.dot(jnp.concatenate(backward, 1), jnp.concatenate(glongs, 0), preferred_element_type=F32)
        )
        crossed = lax.dot_general(
            jnp.concatenate(flips, 0), glong_half, (((1,), (1,)), ((), ())), preferred_element_type=F32
        )
        sums = []
        for g in range(per_half):
            part = jnp.where(linked, crossed[g * TILE : (g + 1) * TILE], 0.0)
            part = pltpu.roll(part, 1, 1, stride=1, stride_axis=0)
            sums.append(jnp.sum(part, 0, keepdims=True))
        med_ref[halves * step + half] = jnp.concatenate(sums, 0)
    long_conv = jnp.concatenate(longs, 1)
    gprod = jnp.concatenate(gprods, 1)
    mixed_ref[...] = jnp.where(living, query * long_conv, 0.0).astype(BF16)

    @pl.when(step >= 2)
    def _():
        for part in range(3):
            store(part, step - 2).wait()

    row8, lane8 = iota((SUB, LANES), 0), iota((SUB, LANES), 1)
    keep = (row8 < 4) == (lane8 < 64)

    def unconv(part, grad, f_ref, taps, shifted):
        sums = [jnp.sum(grad * f_ref[...].astype(F32), 0, keepdims=True)]
        parts = []
        for j in range(1, SHORT):
            sums.append(jnp.sum(grad * shifted[(j - 1) * TILE : j * TILE], 0, keepdims=True))
            parts.append((grad * taps[j : j + 1]).astype(BF16))
        sums.append(jnp.zeros((1, WIDTH), F32))
        sums = jnp.concatenate(sums, 0)
        z = part * (N_Z // 3) + step // 2
        for h in range(halves):
            tile = sums[:, h * LANES : (h + 1) * LANES]
            other = pltpu.roll(pltpu.roll(tile, 64, 1), 4, 0)
            short_ref[z * N_YL + lax.rem(step, 2) * halves + h] = jnp.where(keep, tile, other)
        back = jnp.dot(up_ref[...], jnp.concatenate(parts, 0), preferred_element_type=F32)
        stage_ref[slot, part] = (grad * taps[0:1] + back).astype(BF16)
        store(part, step).start()

    unconv(0, gout * long_conv, fq_ref, q_taps, q_shift)
    unconv(1, gprod * value, fk_ref, k_taps, k_shift)
    unconv(2, gprod * key, fv_ref, v_taps, v_shift)

    @pl.when(step == steps - 1)
    def _():
        medium = jnp.concatenate([med_ref[i] for i in range(2 * halves * 4)], 0).T
        for yl in range(N_YL):
            for core in range(2):
                tiles = [short_ref[z * N_YL + yl][4 * core : 4 * core + 4] for z in range(N_Z)]
                for yh in range(2):
                    to = yh * 2 * N_YL + yl * 2 + core
                    msg_ref[to] = jnp.concatenate(tiles + [medium[to * SUB : (to + 1) * SUB]], 0).astype(BF16)
        for at in (steps - 2, steps - 1):
            for part in range(3):
                store(part, at).wait()


def whole(shape):
    return pl.BlockSpec(shape, lambda *_: (0,) * len(shape))


def tile_call(count, plan, doc_ids, feats, filters, medium, cotangent):
    width = cotangent.shape[1]
    steps = width // WIDTH
    halves = WIDTH // LANES
    groups = medium.shape[1]
    smem = pl.BlockSpec(memory_space=pltpu.SMEM)

    def block(part=0):
        return pl.BlockSpec((TILE, WIDTH), lambda i, part=part: (0, part * steps + i))

    def taps(part):
        return pl.BlockSpec(
            (halves, 1, SUB, LANES), lambda i, part=part: (lax.rem(i, 2), part * (N_Z // 3) + i // 2, 0, 0)
        )

    every = filters.reshape(N_YL * N_Z, SUB, LANES)
    vmem = pltpu.VMEM
    return pl.pallas_call(
        tile_kernel,
        grid=(steps,),
        in_specs=[
            smem, smem, whole((1, TILE)), block(0), block(1), block(2), taps(0), taps(1), taps(2),
            whole(every.shape), whole(medium.shape), block(0),
        ],
        out_specs=[
            block(0), pl.BlockSpec(memory_space=pl.ANY), whole((N_Y, 4 * N_Z + SUB, LANES)),
        ],
        out_shape=[
            jax.ShapeDtypeStruct(cotangent.shape, BF16),
            jax.ShapeDtypeStruct(feats.shape, BF16),
            jax.ShapeDtypeStruct((N_Y, 4 * N_Z + SUB, LANES), BF16),
        ],
        scratch_shapes=[
            vmem(((SHORT - 1) * TILE, TILE), BF16),
            vmem((TILE, (SHORT - 1) * TILE), BF16),
            vmem((TILE, TILE), F32),
            vmem((TILE, TILE), F32),
            vmem((TILE, TILE), BF16),
            vmem((TILE, TILE), F32),
            vmem((TILE, TILE), F32),
            vmem((groups, TILE), F32),
            vmem((groups, TILE), F32),
            vmem((N_Z * N_YL, SUB, LANES), F32),
            vmem((groups // SUB, SUB, TILE), F32),
            vmem((2, 3, TILE, WIDTH), BF16),
            pltpu.SemaphoreType.DMA((2, 3)),
        ],
        name="tile",
    )(count, plan, doc_ids, feats, feats, feats, filters, filters, filters, every, medium, cotangent)


def small_call(kernel, outs, *operands, name):
    in_specs = [
        pl.BlockSpec(memory_space=pltpu.SMEM if x.dtype == jnp.int32 else pltpu.VMEM) for x in operands
    ]
    return pl.pallas_call(
        kernel,
        in_specs=in_specs,
        out_specs=[pl.BlockSpec(memory_space=pltpu.VMEM)] * len(outs),
        out_shape=[jax.ShapeDtypeStruct(*o) for o in outs],
        name=name,
    )(*operands)


def gather_filters(short_filter, counts, plan):
    n_xz = lax.axis_size("x") * N_Z
    lane = iota((SUB, LANES), 1)
    row = iota((SUB, LANES), 0)
    padded = jnp.pad(short_filter, ((0, SUB - SHORT), (0, LANES - short_filter.shape[1])))
    member = jnp.where(lane == plan[0], counts[0], 0).astype(BF16)
    tile = jnp.where(row == SHORT, member, padded)
    got = exchange(jnp.broadcast_to(tile[None], (N_Y, SUB, LANES)), Y)
    where = lax.axis_index("x").astype(jnp.int32).reshape(1)
    (send,) = small_call(pair_kernel, [((n_xz, SUB, LANES), BF16)], where, got, name="pair")
    return exchange(send, XZ).reshape(N_YL, N_Z, SUB, LANES)


def reduce_grads(message):
    n_xz = lax.axis_size("x") * N_Z
    got = exchange(message, Y)
    (send,) = small_call(merge_kernel, [((n_xz, 16, LANES), BF16)], got, name="merge")
    got = exchange(send, XZ)
    short_grad, send = small_call(
        final_kernel, [((SHORT, 64), F32), ((N_Y, SUB, LANES), BF16)], got, name="final"
    )
    return short_grad, exchange(send, Y).reshape(TILE, LANES).astype(F32)


def shards(feats, short_filter, medium_filter, doc_ids, counts, plan, cotangent):
    filters = gather_filters(short_filter, counts, plan)
    mixed, feats_grad, message = tile_call(counts, plan, doc_ids, feats, filters, medium_filter, cotangent)
    short_grad, medium_grad = reduce_grads(message)
    return mixed, feats_grad, short_grad, medium_grad


def solution(mesh):
    parts = Mesh(mesh.devices.reshape([size for _, size in PARTS]), ALL)
    in_specs = (P(ALL, None), P(None, ZERO), P(), P(ALL, None), P(ALL), P(ALL), P(ALL, None))
    out_specs = (P(ALL, None), P(ALL, None), P(None, ZERO), P())
    return jax.shard_map(shards, mesh=parts, in_specs=in_specs, out_specs=out_specs, check_vma=False)
```

```python
import jax
import jax.numpy as jnp
from jax import lax
from jax.experimental import pallas as pl
from jax.experimental.pallas import tpu as pltpu
from jax.sharding import Mesh, PartitionSpec as P

SHORT = 7
TILE = 128
LANES = 128
WIDTH = 512
PER_Z = 512 // WIDTH
GSIZE = 16
SUB = 8
RANKS = 8
F32, BF16 = jnp.float32, jnp.bfloat16

PARTS = (("y_hi", 2), ("x_hi", 2), ("x_lo", 2), ("z", 12), ("y_lo", 4), ("core", 2))
Y = ("y_hi", "y_lo", "core")
X = ("x_hi", "x_lo")
XZ = X + ("z",)
SHARE = ("x_lo",) + Y
ALL = tuple(name for name, _ in PARTS)
ZERO = ("z", "y_lo", "core")
N_Y = 16
N_Z = 12
N_YL = 4
N_X = 4


def iota(shape, dim):
    return lax.broadcasted_iota(jnp.int32, shape, dim)


def exchange(values, axes):
    return lax.all_to_all(values, axes, 0, 0, tiled=True)


def pair_kernel(x_ref, got_ref, out_ref):
    lane = iota((SUB, LANES), 1)
    row = iota((SUB, LANES), 0)
    tiles = [got_ref[i].astype(F32) for i in range(N_Y)]
    live = tiles[0]
    for tile in tiles[1:]:
        live = live + tile
    high = jnp.floor(live * (1.0 / 64.0))
    low = pltpu.roll(live - 64.0 * high, SUB, 1)
    live = jnp.where(lane < SUB, high, jnp.where(lane < 2 * SUB, low, 0.0))
    out = jnp.zeros((SUB, LANES), F32)
    for yl in range(N_YL):
        both = jnp.where(lane < 64, tiles[2 * yl], pltpu.roll(tiles[2 * yl + 1], 64, 1))
        out = jnp.where(x_ref[0] == yl, both, out)
    out = jnp.where(row == SHORT, live, out).astype(BF16)
    for i in range(out_ref.shape[0]):
        out_ref[i] = out


def merge_kernel(got_ref, out_ref):
    total = got_ref[0].astype(F32)
    for i in range(1, N_Y):
        total = total + got_ref[i].astype(F32)
    for xl in range(2):
        medium = total[4 * N_Z + 4 * xl : 4 * N_Z + 4 * xl + 4]
        for z in range(N_Z):
            tile = jnp.concatenate([total[4 * z : 4 * z + 4], medium], 0).astype(BF16)
            for xh in range(N_X // 2):
                out_ref[(2 * xh + xl) * N_Z + z] = tile


def final_kernel(got_ref, short_ref, out_ref):
    total = got_ref[0].astype(F32)
    for i in range(1, got_ref.shape[0]):
        total = total + got_ref[i].astype(F32)
    short_ref[0:4, :] = total[0:4, :64]
    short_ref[4:SHORT, :] = total[0 : SHORT - 4, 64:]
    medium = total[4:]
    for i in range(out_ref.shape[0]):
        out_ref[i] = medium


def prepare_kernel(seg_ref, medium_ref, down_ref, up_ref, linked_ref, forward_ref, backward_ref, taps_ref, rtaps_ref):
    rows, cols = iota((TILE, TILE), 0), iota((TILE, TILE), 1)
    along = jnp.broadcast_to(seg_ref[...].astype(F32), (TILE, TILE))
    same = along == along.T
    lower, upper = same & (rows >= cols), same & (rows <= cols)

    @pl.when(pl.program_id(0) == 0)
    def _():
        for j in range(1, SHORT):
            down_ref[pl.ds((j - 1) * TILE, TILE), :] = jnp.where(same & (rows - cols == j), 1.0, 0.0).astype(BF16)
            up_ref[pl.ds((j - 1) * TILE, TILE), :] = jnp.where(same & (cols - rows == j), 1.0, 0.0).astype(BF16)
        flip = jnp.where(rows + cols == TILE - 1, 1.0, 0.0).astype(BF16)
        down_ref[pl.ds((SHORT - 1) * TILE, TILE), :] = flip
        linked_ref[...] = jnp.dot(flip, jnp.where(upper, 1.0, 0.0).astype(BF16), preferred_element_type=F32)
        taps = medium_ref[...].T.astype(BF16)
        taps_ref[...] = taps.astype(F32)
        rtaps_ref[...] = pltpu.roll(jnp.dot(taps, flip, preferred_element_type=F32), 1, 1)

    n = forward_ref.shape[1] // TILE
    at = pl.ds(pl.multiple_of(pl.program_id(0) * n, n), n)
    taps, rtaps = taps_ref[at, :], rtaps_ref[at, :]
    for g in range(n):
        where = slice(g * TILE, (g + 1) * TILE)
        base = jnp.broadcast_to(rtaps[g : g + 1, :], (TILE, TILE))
        base = pltpu.roll(base, 0, 1, stride=1, stride_axis=0)
        forward_ref[:, where] = jnp.where(lower, base, 0.0).astype(BF16)
        base = jnp.broadcast_to(taps[g : g + 1, :], (TILE, TILE))
        base = pltpu.roll(base, 0, 1, stride=1, stride_axis=0)
        backward_ref[:, where] = jnp.where(upper, base, 0.0).astype(BF16)


def tile_kernel(
    count_ref, plan_ref, fq_ref, fk_ref, fv_ref, sq_ref, sk_ref, sv_ref,
    every_ref, down_ref, linked_ref, forward_ref, backward_ref, cot_ref,
    mixed_ref, gq_ref, gk_ref, gv_ref, msg_ref,
    scale_ref, short_ref, med_ref,
):
    rows = iota((TILE, TILE), 0)
    step, steps = pl.program_id(0), pl.num_programs(0)
    halves = WIDTH // LANES
    per_half = LANES // GSIZE

    @pl.when(step == 0)
    def _():
        live = every_ref[0].astype(F32)
        for i in range(1, every_ref.shape[0]):
            live = live + every_ref[i].astype(F32)
        row8, lane8 = iota((SUB, LANES), 0), iota((SUB, LANES), 1)
        high = jnp.where((row8 == SHORT) & (lane8 == plan_ref[0]), 64.0 * live, 0.0)
        low = jnp.where((row8 == SHORT) & (lane8 == plan_ref[0] + RANKS), live, 0.0)
        total = jnp.sum(jnp.sum(high + low, 0, keepdims=True), 1, keepdims=True)
        tiles = every_ref.shape[0] * N_Y
        weighting = (TILE * tiles / RANKS) / jnp.broadcast_to(total, (TILE, TILE))
        scale_ref[...] = jnp.where(rows < count_ref[0], weighting, 0.0)

    linked = linked_ref[...] > 0.5
    scale = jnp.concatenate([scale_ref[...]] * halves, 1)
    living = iota((TILE, WIDTH), 0) < count_ref[0]
    lane_group = iota((TILE, LANES), 1) // GSIZE

    def conv(f_ref, s_ref):
        feats = f_ref[...]
        taps = jnp.concatenate([s_ref[h, 0].astype(F32) for h in range(halves)], 1)
        shifted = jnp.dot(down_ref[: (SHORT - 1) * TILE], feats, preferred_element_type=F32)
        total = feats.astype(F32) * taps[0:1]
        for j in range(1, SHORT):
            total = total + shifted[(j - 1) * TILE : j * TILE] * taps[j : j + 1]
        return total, shifted

    query, q_shift = conv(fq_ref, sq_ref)
    key, k_shift = conv(fk_ref, sk_ref)
    value, v_shift = conv(fv_ref, sv_ref)
    product = (key * value).astype(BF16)
    flipped = jnp.dot(down_ref[(SHORT - 1) * TILE :], product, preferred_element_type=F32).astype(BF16)
    gout = cot_ref[...].astype(F32) * scale
    glong = (gout * query).astype(BF16)
    zero = jnp.zeros((TILE, LANES), BF16)

    longs, gprods = [], []
    for half in range(halves):
        lanes = slice(half * LANES, (half + 1) * LANES)
        blocks = slice(half * per_half * TILE, (half + 1) * per_half * TILE)
        prod_half, glong_half, flip_half = product[:, lanes], glong[:, lanes], flipped[:, lanes]
        prods, glongs, flips = [], [], []
        for g in range(per_half):
            prods.append(jnp.where(lane_group == g, prod_half, zero))
            glongs.append(jnp.where(lane_group == g, glong_half, zero))
            flips.append(jnp.where(lane_group == g, flip_half, zero))
        longs.append(jnp.dot(forward_ref[:, blocks], jnp.concatenate(prods, 0), preferred_element_type=F32))
        gprods.append(jnp.dot(backward_ref[:, blocks], jnp.concatenate(glongs, 0), preferred_element_type=F32))
        crossed = lax.dot_general(
            jnp.concatenate(flips, 0), glong_half, (((1,), (1,)), ((), ())), preferred_element_type=F32
        )
        sums = []
        for g in range(per_half):
            part = jnp.where(linked, crossed[g * TILE : (g + 1) * TILE], 0.0)
            part = pltpu.roll(part, 1, 1, stride=1, stride_axis=0)
            sums.append(jnp.sum(part, 0, keepdims=True))
        med_ref[halves * step + half] = jnp.concatenate(sums, 0)
    long_conv = jnp.concatenate(longs, 1)
    gprod = jnp.concatenate(gprods, 1)
    mixed_ref[...] = jnp.where(living, query * long_conv, 0.0).astype(BF16)

    row8, lane8 = iota((SUB, LANES), 0), iota((SUB, LANES), 1)
    keep = (row8 < 4) == (lane8 < 64)

    def taps_grad(part, grad, f_ref, shifted, g_ref):
        g_ref[...] = grad.astype(BF16)
        sums = [jnp.sum(grad * f_ref[...].astype(F32), 0, keepdims=True)]
        for j in range(1, SHORT):
            sums.append(jnp.sum(grad * shifted[(j - 1) * TILE : j * TILE], 0, keepdims=True))
        sums.append(jnp.zeros((1, WIDTH), F32))
        sums = jnp.concatenate(sums, 0)
        z = part * (N_Z // 3) + step // PER_Z
        for h in range(halves):
            tile = sums[:, h * LANES : (h + 1) * LANES]
            other = pltpu.roll(pltpu.roll(tile, 64, 1), 4, 0)
            short_ref[z * N_YL + lax.rem(step, PER_Z) * halves + h] = jnp.where(keep, tile, other)

    taps_grad(0, gout * long_conv, fq_ref, q_shift, gq_ref)
    taps_grad(1, gprod * value, fk_ref, k_shift, gk_ref)
    taps_grad(2, gprod * key, fv_ref, v_shift, gv_ref)

    @pl.when(step == steps - 1)
    def _():
        medium = jnp.concatenate([med_ref[i] for i in range(med_ref.shape[0])], 0).T
        for yl in range(N_YL):
            for core in range(2):
                tiles = [short_ref[z * N_YL + yl][4 * core : 4 * core + 4] for z in range(N_Z)]
                for yh in range(2):
                    to = yh * 2 * N_YL + yl * 2 + core
                    pieces = [medium[64 * xl + 4 * to : 64 * xl + 4 * to + 4] for xl in range(2)]
                    msg_ref[to] = jnp.concatenate(tiles + pieces, 0).astype(BF16)


def spread_kernel(gq_ref, gk_ref, gv_ref, sq_ref, sk_ref, sv_ref, up_ref, dfeats_ref, stage_ref, sems):
    step, steps = pl.program_id(0), pl.num_programs(0)
    width = gq_ref.shape[1]

    def store(part, at):
        where = pl.multiple_of((part * steps + at) * width, width)
        return pltpu.make_async_copy(
            stage_ref.at[lax.rem(at, 2), part], dfeats_ref.at[:, pl.ds(where, width)], sems.at[lax.rem(at, 2), part]
        )

    @pl.when(step >= 2)
    def _():
        for part in range(3):
            store(part, step - 2).wait()

    for part, (g_ref, s_ref) in enumerate(((gq_ref, sq_ref), (gk_ref, sk_ref), (gv_ref, sv_ref))):
        grad = g_ref[...]
        taps = jnp.concatenate([s_ref[h, 0].astype(F32) for h in range(s_ref.shape[0])], 1)
        shifted = jnp.dot(up_ref[...], grad, preferred_element_type=F32)
        total = grad.astype(F32) * taps[0:1]
        for j in range(1, SHORT):
            total = total + shifted[(j - 1) * TILE : j * TILE] * taps[j : j + 1]
        stage_ref[lax.rem(step, 2), part] = total.astype(BF16)
        store(part, step).start()

    @pl.when(step == steps - 1)
    def _():
        for at in (steps - 2, steps - 1):
            for part in range(3):
                store(part, at).wait()


def whole(shape):
    return pl.BlockSpec(shape, lambda *_: (0,) * len(shape))


def block(rows=TILE, part=0, steps=0):
    return pl.BlockSpec((rows, WIDTH), lambda i: (0, part * steps + i))


def taps_block(part):
    return pl.BlockSpec((WIDTH // LANES, 1, SUB, LANES), lambda i: (lax.rem(i, PER_Z), part * (N_Z // 3) + i // PER_Z, 0, 0))


SMEM = pl.BlockSpec(memory_space=pltpu.SMEM)


def prepare_call(doc_ids, medium):
    groups = medium.shape[1]
    n = 16
    rows = pl.BlockSpec((TILE, n * TILE), lambda i: (0, i))
    return pl.pallas_call(
        prepare_kernel,
        grid=(groups // n,),
        in_specs=[whole((1, TILE)), whole(medium.shape)],
        out_specs=[whole((SHORT * TILE, TILE)), whole(((SHORT - 1) * TILE, TILE)), whole((TILE, TILE)), rows, rows],
        out_shape=[
            jax.ShapeDtypeStruct((SHORT * TILE, TILE), BF16),
            jax.ShapeDtypeStruct(((SHORT - 1) * TILE, TILE), BF16),
            jax.ShapeDtypeStruct((TILE, TILE), F32),
            jax.ShapeDtypeStruct((TILE, groups * TILE), BF16),
            jax.ShapeDtypeStruct((TILE, groups * TILE), BF16),
        ],
        scratch_shapes=[pltpu.VMEM((groups, TILE), F32), pltpu.VMEM((groups, TILE), F32)],
        name="prepare",
    )(doc_ids, medium)


def tile_call(count, plan, feats, filters, down, linked, forward, backward, cotangent):
    width = cotangent.shape[1]
    steps = width // WIDTH
    every = filters.reshape(N_YL * N_Z, SUB, LANES)
    toeplitz = pl.BlockSpec((TILE, forward.shape[1] // steps), lambda i: (0, i))
    message = (N_Y, 4 * N_Z + SUB, LANES)
    vmem = pltpu.VMEM
    part = jax.ShapeDtypeStruct(cotangent.shape, BF16)
    return pl.pallas_call(
        tile_kernel,
        grid=(steps,),
        in_specs=[SMEM, SMEM]
        + [block(TILE, p, steps) for p in range(3)]
        + [taps_block(p) for p in range(3)]
        + [whole(every.shape), whole(down.shape), whole(linked.shape), toeplitz, toeplitz, block()],
        out_specs=[block(), block(), block(), block(), whole(message)],
        out_shape=[part, part, part, part, jax.ShapeDtypeStruct(message, BF16)],
        scratch_shapes=[
            vmem((TILE, TILE), F32),
            vmem((N_Z * N_YL, SUB, LANES), F32),
            vmem((forward.shape[1] // TILE // SUB, SUB, TILE), F32),
        ],
        name="tile",
    )(count, plan, feats, feats, feats, filters, filters, filters, every, down, linked, forward, backward, cotangent)


def spread_call(grads, filters, up):
    width = grads[0].shape[1]
    steps = width // WIDTH
    return pl.pallas_call(
        spread_kernel,
        grid=(steps,),
        in_specs=[block()] * 3 + [taps_block(p) for p in range(3)] + [whole(up.shape)],
        out_specs=pl.BlockSpec(memory_space=pl.ANY),
        out_shape=jax.ShapeDtypeStruct((TILE, 3 * width), BF16),
        scratch_shapes=[pltpu.VMEM((2, 3, TILE, WIDTH), BF16), pltpu.SemaphoreType.DMA((2, 3))],
        name="spread",
    )(*grads, filters, filters, filters, up)


def small_call(kernel, outs, *operands):
    in_specs = [
        pl.BlockSpec(memory_space=pltpu.SMEM if x.dtype == jnp.int32 else pltpu.VMEM) for x in operands
    ]
    return pl.pallas_call(
        kernel,
        in_specs=in_specs,
        out_specs=[pl.BlockSpec(memory_space=pltpu.VMEM)] * len(outs),
        out_shape=[jax.ShapeDtypeStruct(*o) for o in outs],
    )(*operands)


def gather_filters(short_filter, counts, plan):
    n_xz = N_X * N_Z
    lane = iota((SUB, LANES), 1)
    row = iota((SUB, LANES), 0)
    padded = jnp.pad(short_filter, ((0, SUB - SHORT), (0, LANES - short_filter.shape[1])))
    member = jnp.where(lane == plan[0], counts[0], 0).astype(BF16)
    tile = jnp.where(row == SHORT, member, padded)
    got = exchange(jnp.broadcast_to(tile[None], (N_Y, SUB, LANES)), Y)
    where = lax.axis_index(X).astype(jnp.int32).reshape(1)
    (send,) = small_call(pair_kernel, [((n_xz, SUB, LANES), BF16)], where, got)
    return exchange(send, XZ).reshape(N_YL, N_Z, SUB, LANES)


def reduce_grads(message):
    n_xz = N_X * N_Z
    got = exchange(message, Y)
    (send,) = small_call(merge_kernel, [((n_xz, SUB, LANES), BF16)], got)
    got = exchange(send, XZ)
    short_grad, send = small_call(final_kernel, [((SHORT, 64), F32), ((2 * N_Y, 4, LANES), F32)], got)
    return short_grad, exchange(send, SHARE).reshape(TILE, LANES)


def shards(feats, short_filter, medium_filter, doc_ids, counts, plan, cotangent):
    down, up, linked, forward, backward = prepare_call(doc_ids, medium_filter)
    filters = gather_filters(short_filter, counts, plan)
    mixed, gq, gk, gv, message = tile_call(
        counts, plan, feats, filters, down, linked, forward, backward, cotangent
    )
    feats_grad = spread_call((gq, gk, gv), filters, up)
    short_grad, medium_grad = reduce_grads(message)
    return mixed, feats_grad, short_grad, medium_grad


def solution(mesh):
    parts = Mesh(mesh.devices.reshape([size for _, size in PARTS]), ALL)
    in_specs = (P(ALL, None), P(None, ZERO), P(), P(ALL, None), P(ALL), P(ALL), P(ALL, None))
    out_specs = (P(ALL, None), P(ALL, None), P(None, ZERO), P())
    return jax.shard_map(shards, mesh=parts, in_specs=in_specs, out_specs=out_specs, check_vma=False)
```

```python
import jax
import jax.numpy as jnp
from jax import lax
from jax.experimental import pallas as pl
from jax.experimental.pallas import tpu as pltpu
from jax.sharding import Mesh, PartitionSpec as P

SHORT = 7
TILE = 128
LANES = 128
WIDTH = 512
PER_STEP = WIDTH // 512
GSIZE = 16
SUB = 8
RANKS = 8
F32, BF16 = jnp.float32, jnp.bfloat16

PARTS = (("y_hi", 2), ("x_hi", 2), ("x_lo", 2), ("z", 12), ("y_lo", 4), ("core", 2))
Y = ("y_hi", "y_lo", "core")
X = ("x_hi", "x_lo")
XZ = X + ("z",)
SHARE = ("x_lo",) + Y
ALL = tuple(name for name, _ in PARTS)
ZERO = ("z", "y_lo", "core")
N_Y = 16
N_Z = 12
N_YL = 4
N_X = 4


def iota(shape, dim):
    return lax.broadcasted_iota(jnp.int32, shape, dim)


def exchange(values, axes):
    return lax.all_to_all(values, axes, 0, 0, tiled=True)


def first_kernel(count_ref, plan_ref, filter_ref, out_ref, tile_ref):
    lane = iota((SUB, LANES), 1)
    row = iota((SUB, LANES), 0)
    tile_ref[...] = jnp.zeros((SUB, LANES), F32)
    tile_ref[0:SHORT, 0:64] = filter_ref[...].astype(F32)
    live = jnp.where(lane == plan_ref[0], count_ref[0].astype(F32), 0.0)
    tile = jnp.where(row == SHORT, live, tile_ref[...]).astype(BF16)
    for i in range(out_ref.shape[0]):
        out_ref[i] = tile


def pair_kernel(x_ref, got_ref, out_ref):
    lane = iota((SUB, LANES), 1)
    row = iota((SUB, LANES), 0)
    tiles = [got_ref[i].astype(F32) for i in range(N_Y)]
    live = tiles[0]
    for tile in tiles[1:]:
        live = live + tile
    high = jnp.floor(live * (1.0 / 64.0))
    low = pltpu.roll(live - 64.0 * high, SUB, 1)
    live = jnp.where(lane < SUB, high, jnp.where(lane < 2 * SUB, low, 0.0))
    out = jnp.zeros((SUB, LANES), F32)
    for yl in range(N_YL):
        both = jnp.where(lane < 64, tiles[2 * yl], pltpu.roll(tiles[2 * yl + 1], 64, 1))
        out = jnp.where(x_ref[0] == yl, both, out)
    out = jnp.where(row == SHORT, live, out).astype(BF16)
    for i in range(out_ref.shape[0]):
        out_ref[i] = out


def merge_kernel(got_ref, out_ref):
    total = got_ref[0].astype(F32)
    for i in range(1, N_Y):
        total = total + got_ref[i].astype(F32)
    for xl in range(2):
        medium = total[4 * N_Z + 4 * xl : 4 * N_Z + 4 * xl + 4]
        for z in range(N_Z):
            tile = jnp.concatenate([total[4 * z : 4 * z + 4], medium], 0).astype(BF16)
            for xh in range(N_X // 2):
                out_ref[(2 * xh + xl) * N_Z + z] = tile


def final_kernel(got_ref, short_ref, out_ref):
    total = got_ref[0].astype(F32)
    for i in range(1, got_ref.shape[0]):
        total = total + got_ref[i].astype(F32)
    short_ref[0:4, :] = total[0:4, :64]
    short_ref[4:SHORT, :] = total[0 : SHORT - 4, 64:]
    medium = total[4:]
    for i in range(out_ref.shape[0]):
        out_ref[i] = medium


def prepare_kernel(seg_ref, medium_ref, down_ref, up_ref, linked_ref, forward_ref, backward_ref, taps_ref, rtaps_ref):
    rows, cols = iota((TILE, TILE), 0), iota((TILE, TILE), 1)
    along = jnp.broadcast_to(seg_ref[...].astype(F32), (TILE, TILE))
    same = along == along.T
    lower, upper = same & (rows >= cols), same & (rows <= cols)

    @pl.when(pl.program_id(0) == 0)
    def _():
        for j in range(1, SHORT):
            down_ref[pl.ds((j - 1) * TILE, TILE), :] = jnp.where(same & (rows - cols == j), 1.0, 0.0).astype(BF16)
            up_ref[pl.ds((j - 1) * TILE, TILE), :] = jnp.where(same & (cols - rows == j), 1.0, 0.0).astype(BF16)
        flip = jnp.where(rows + cols == TILE - 1, 1.0, 0.0).astype(BF16)
        down_ref[pl.ds((SHORT - 1) * TILE, TILE), :] = flip
        linked_ref[...] = jnp.dot(flip, jnp.where(upper, 1.0, 0.0).astype(BF16), preferred_element_type=F32)
        taps = medium_ref[...].T.astype(BF16)
        taps_ref[...] = taps.astype(F32)
        rtaps_ref[...] = pltpu.roll(jnp.dot(taps, flip, preferred_element_type=F32), 1, 1)

    n = forward_ref.shape[1] // TILE
    at = pl.ds(pl.multiple_of(pl.program_id(0) * n, n), n)
    taps, rtaps = taps_ref[at, :], rtaps_ref[at, :]
    for g in range(n):
        where = slice(g * TILE, (g + 1) * TILE)
        base = jnp.broadcast_to(rtaps[g : g + 1, :], (TILE, TILE))
        base = pltpu.roll(base, 0, 1, stride=1, stride_axis=0)
        forward_ref[:, where] = jnp.where(lower, base, 0.0).astype(BF16)
        base = jnp.broadcast_to(taps[g : g + 1, :], (TILE, TILE))
        base = pltpu.roll(base, 0, 1, stride=1, stride_axis=0)
        backward_ref[:, where] = jnp.where(upper, base, 0.0).astype(BF16)


def taps_here(every_ref, part, step):
    tiles = []
    for h in range(WIDTH // LANES):
        z = part * (N_Z // 3) + step * PER_STEP + h // N_YL
        tiles.append(every_ref[(h % N_YL) * N_Z + z].astype(F32))
    return jnp.concatenate(tiles, 1)


def tile_kernel(
    count_ref, plan_ref, fq_ref, fk_ref, fv_ref, every_ref, down_ref, linked_ref, forward_ref, backward_ref, cot_ref,
    mixed_ref, gq_ref, gk_ref, gv_ref, msg_ref,
    scale_ref, short_ref, med_ref,
):
    rows = iota((TILE, TILE), 0)
    step, steps = pl.program_id(0), pl.num_programs(0)
    halves = WIDTH // LANES
    per_half = LANES // GSIZE

    @pl.when(step == 0)
    def _():
        live = every_ref[0].astype(F32)
        for i in range(1, every_ref.shape[0]):
            live = live + every_ref[i].astype(F32)
        row8, lane8 = iota((SUB, LANES), 0), iota((SUB, LANES), 1)
        high = jnp.where((row8 == SHORT) & (lane8 == plan_ref[0]), 64.0 * live, 0.0)
        low = jnp.where((row8 == SHORT) & (lane8 == plan_ref[0] + RANKS), live, 0.0)
        total = jnp.sum(jnp.sum(high + low, 0, keepdims=True), 1, keepdims=True)
        tiles = every_ref.shape[0] * N_Y
        weighting = (TILE * tiles / RANKS) / jnp.broadcast_to(total, (TILE, TILE))
        scale_ref[...] = jnp.where(rows < count_ref[0], weighting, 0.0)

    linked = linked_ref[...] > 0.5
    scale = jnp.concatenate([scale_ref[...]] * halves, 1)
    living = iota((TILE, WIDTH), 0) < count_ref[0]
    lane_group = iota((TILE, LANES), 1) // GSIZE

    def conv(part, f_ref):
        feats = f_ref[...]
        taps = taps_here(every_ref, part, step)
        shifted = jnp.dot(down_ref[: (SHORT - 1) * TILE], feats, preferred_element_type=F32)
        total = feats.astype(F32) * taps[0:1]
        for j in range(1, SHORT):
            total = total + shifted[(j - 1) * TILE : j * TILE] * taps[j : j + 1]
        return total, shifted

    query, q_shift = conv(0, fq_ref)
    key, k_shift = conv(1, fk_ref)
    value, v_shift = conv(2, fv_ref)
    product = (key * value).astype(BF16)
    flipped = jnp.dot(down_ref[(SHORT - 1) * TILE :], product, preferred_element_type=F32).astype(BF16)
    gout = cot_ref[...].astype(F32) * scale
    glong = (gout * query).astype(BF16)
    zero = jnp.zeros((TILE, LANES), BF16)

    longs, gprods = [], []
    for half in range(halves):
        lanes = slice(half * LANES, (half + 1) * LANES)
        blocks = slice(half * per_half * TILE, (half + 1) * per_half * TILE)
        prod_half, glong_half, flip_half = product[:, lanes], glong[:, lanes], flipped[:, lanes]
        prods, glongs, flips = [], [], []
        for g in range(per_half):
            prods.append(jnp.where(lane_group == g, prod_half, zero))
            glongs.append(jnp.where(lane_group == g, glong_half, zero))
            flips.append(jnp.where(lane_group == g, flip_half, zero))
        longs.append(jnp.dot(forward_ref[:, blocks], jnp.concatenate(prods, 0), preferred_element_type=F32))
        gprods.append(jnp.dot(backward_ref[:, blocks], jnp.concatenate(glongs, 0), preferred_element_type=F32))
        crossed = lax.dot_general(
            jnp.concatenate(flips, 0), glong_half, (((1,), (1,)), ((), ())), preferred_element_type=F32
        )
        sums = []
        for g in range(per_half):
            part = jnp.where(linked, crossed[g * TILE : (g + 1) * TILE], 0.0)
            part = pltpu.roll(part, 1, 1, stride=1, stride_axis=0)
            sums.append(jnp.sum(part, 0, keepdims=True))
        med_ref[halves * step + half] = jnp.concatenate(sums, 0)
    long_conv = jnp.concatenate(longs, 1)
    gprod = jnp.concatenate(gprods, 1)
    mixed_ref[...] = jnp.where(living, query * long_conv, 0.0).astype(BF16)

    row8, lane8 = iota((SUB, LANES), 0), iota((SUB, LANES), 1)
    keep = (row8 < 4) == (lane8 < 64)

    def taps_grad(part, grad, f_ref, shifted, g_ref):
        g_ref[...] = grad.astype(BF16)
        sums = [jnp.sum(grad * f_ref[...].astype(F32), 0, keepdims=True)]
        for j in range(1, SHORT):
            sums.append(jnp.sum(grad * shifted[(j - 1) * TILE : j * TILE], 0, keepdims=True))
        sums.append(jnp.zeros((1, WIDTH), F32))
        sums = jnp.concatenate(sums, 0)
        for h in range(halves):
            tile = sums[:, h * LANES : (h + 1) * LANES]
            other = pltpu.roll(pltpu.roll(tile, 64, 1), 4, 0)
            z = part * (N_Z // 3) + step * PER_STEP + h // N_YL
            short_ref[z * N_YL + h % N_YL] = jnp.where(keep, tile, other)

    taps_grad(0, gout * long_conv, fq_ref, q_shift, gq_ref)
    taps_grad(1, gprod * value, fk_ref, k_shift, gk_ref)
    taps_grad(2, gprod * key, fv_ref, v_shift, gv_ref)

    @pl.when(step == steps - 1)
    def _():
        medium = jnp.concatenate([med_ref[i] for i in range(med_ref.shape[0])], 0).T
        for yl in range(N_YL):
            for core in range(2):
                tiles = [short_ref[z * N_YL + yl][4 * core : 4 * core + 4] for z in range(N_Z)]
                for yh in range(2):
                    to = yh * 2 * N_YL + yl * 2 + core
                    pieces = [medium[64 * xl + 4 * to : 64 * xl + 4 * to + 4] for xl in range(2)]
                    msg_ref[to] = jnp.concatenate(tiles + pieces, 0).astype(BF16)


def spread_kernel(gq_ref, gk_ref, gv_ref, every_ref, up_ref, dfeats_ref, stage_ref, sems):
    step, steps = pl.program_id(0), pl.num_programs(0)
    width = gq_ref.shape[1]

    def store(part, at):
        where = pl.multiple_of((part * steps + at) * width, width)
        return pltpu.make_async_copy(
            stage_ref.at[lax.rem(at, 2), part], dfeats_ref.at[:, pl.ds(where, width)], sems.at[lax.rem(at, 2), part]
        )

    @pl.when(step >= 2)
    def _():
        for part in range(3):
            store(part, step - 2).wait()

    for part, g_ref in enumerate((gq_ref, gk_ref, gv_ref)):
        grad = g_ref[...]
        taps = taps_here(every_ref, part, step)
        shifted = jnp.dot(up_ref[...], grad, preferred_element_type=F32)
        total = grad.astype(F32) * taps[0:1]
        for j in range(1, SHORT):
            total = total + shifted[(j - 1) * TILE : j * TILE] * taps[j : j + 1]
        stage_ref[lax.rem(step, 2), part] = total.astype(BF16)
        store(part, step).start()

    @pl.when(step == steps - 1)
    def _():
        for at in (steps - 2, steps - 1):
            for part in range(3):
                store(part, at).wait()


def whole(shape):
    return pl.BlockSpec(shape, lambda *_: (0,) * len(shape))


def block(rows=TILE, part=0, steps=0):
    return pl.BlockSpec((rows, WIDTH), lambda i: (0, part * steps + i))


SMEM = pl.BlockSpec(memory_space=pltpu.SMEM)
VMEM = pl.BlockSpec(memory_space=pltpu.VMEM)


def prepare_call(doc_ids, medium):
    groups = medium.shape[1]
    n = 16
    rows = pl.BlockSpec((TILE, n * TILE), lambda i: (0, i))
    return pl.pallas_call(
        prepare_kernel,
        grid=(groups // n,),
        in_specs=[whole((1, TILE)), whole(medium.shape)],
        out_specs=[whole((SHORT * TILE, TILE)), whole(((SHORT - 1) * TILE, TILE)), whole((TILE, TILE)), rows, rows],
        out_shape=[
            jax.ShapeDtypeStruct((SHORT * TILE, TILE), BF16),
            jax.ShapeDtypeStruct(((SHORT - 1) * TILE, TILE), BF16),
            jax.ShapeDtypeStruct((TILE, TILE), F32),
            jax.ShapeDtypeStruct((TILE, groups * TILE), BF16),
            jax.ShapeDtypeStruct((TILE, groups * TILE), BF16),
        ],
        scratch_shapes=[pltpu.VMEM((groups, TILE), F32), pltpu.VMEM((groups, TILE), F32)],
        name="prepare",
    )(doc_ids, medium)


def tile_call(count, plan, feats, filters, down, linked, forward, backward, cotangent):
    width = cotangent.shape[1]
    steps = width // WIDTH
    toeplitz = pl.BlockSpec((TILE, forward.shape[1] // steps), lambda i: (0, i))
    message = (N_Y, 4 * N_Z + SUB, LANES)
    vmem = pltpu.VMEM
    part = jax.ShapeDtypeStruct(cotangent.shape, BF16)
    return pl.pallas_call(
        tile_kernel,
        grid=(steps,),
        in_specs=[SMEM, SMEM]
        + [block(TILE, p, steps) for p in range(3)]
        + [VMEM, whole(down.shape), whole(linked.shape), toeplitz, toeplitz, block()],
        out_specs=[block(), block(), block(), block(), VMEM],
        out_shape=[part, part, part, part, pltpu.VMEM(message, BF16)],
        scratch_shapes=[
            vmem((TILE, TILE), F32),
            vmem((N_Z * N_YL, SUB, LANES), F32),
            vmem((forward.shape[1] // TILE // SUB, SUB, TILE), F32),
        ],
        name="tile",
    )(count, plan, feats, feats, feats, filters, down, linked, forward, backward, cotangent)


def spread_call(grads, filters, up):
    width = grads[0].shape[1]
    steps = width // WIDTH
    return pl.pallas_call(
        spread_kernel,
        grid=(steps,),
        in_specs=[block()] * 3 + [VMEM, whole(up.shape)],
        out_specs=pl.BlockSpec(memory_space=pl.ANY),
        out_shape=jax.ShapeDtypeStruct((TILE, 3 * width), BF16),
        scratch_shapes=[pltpu.VMEM((2, 3, TILE, WIDTH), BF16), pltpu.SemaphoreType.DMA((2, 3))],
        name="spread",
    )(*grads, filters, up)


def small_call(kernel, outs, *operands, scratch=()):
    in_specs = [
        pl.BlockSpec(memory_space=pltpu.SMEM if x.dtype == jnp.int32 else pltpu.VMEM) for x in operands
    ]
    operands = [
        x if x.dtype == jnp.int32 else pltpu.with_memory_space_constraint(x, pltpu.VMEM) for x in operands
    ]
    return pl.pallas_call(
        kernel,
        in_specs=in_specs,
        out_specs=[pl.BlockSpec(memory_space=pltpu.VMEM)] * len(outs),
        out_shape=[pltpu.VMEM(*o) if keep else jax.ShapeDtypeStruct(*o) for keep, *o in outs],
        scratch_shapes=scratch,
    )(*operands)


def gather_filters(short_filter, counts, plan):
    n_xz = N_X * N_Z
    (send,) = small_call(
        first_kernel, [(False, (N_Y, SUB, LANES), BF16)], counts, plan, short_filter,
        scratch=[pltpu.VMEM((SUB, LANES), F32)],
    )
    got = exchange(send, Y)
    where = lax.axis_index(X).astype(jnp.int32).reshape(1)
    (send,) = small_call(pair_kernel, [(True, (n_xz, SUB, LANES), BF16)], where, got)
    return pltpu.with_memory_space_constraint(exchange(send, XZ), pltpu.VMEM)


def reduce_grads(message):
    n_xz = N_X * N_Z
    got = exchange(message, Y)
    (send,) = small_call(merge_kernel, [(True, (n_xz, SUB, LANES), BF16)], got)
    got = exchange(send, XZ)
    short_grad, send = small_call(final_kernel, [(False, (SHORT, 64), F32), (True, (2 * N_Y, 4, LANES), F32)], got)
    return short_grad, exchange(send, SHARE).reshape(TILE, LANES)


def shards(feats, short_filter, medium_filter, doc_ids, counts, plan, cotangent):
    down, up, linked, forward, backward = prepare_call(doc_ids, medium_filter)
    filters = gather_filters(short_filter, counts, plan)
    mixed, gq, gk, gv, message = tile_call(
        counts, plan, feats, filters, down, linked, forward, backward, cotangent
    )
    feats_grad = spread_call((gq, gk, gv), filters, up)
    short_grad, medium_grad = reduce_grads(message)
    return mixed, feats_grad, short_grad, medium_grad


def solution(mesh):
    parts = Mesh(mesh.devices.reshape([size for _, size in PARTS]), ALL)
    in_specs = (P(ALL, None), P(None, ZERO), P(), P(ALL, None), P(ALL), P(ALL), P(ALL, None))
    out_specs = (P(ALL, None), P(ALL, None), P(None, ZERO), P())
    return jax.shard_map(shards, mesh=parts, in_specs=in_specs, out_specs=out_specs, check_vma=False)
```

```python
import jax
import jax.numpy as jnp
from jax import lax
from jax.experimental import pallas as pl
from jax.experimental.pallas import tpu as pltpu
from jax.sharding import Mesh, PartitionSpec as P

SHORT = 7
TILE = 128
LANES = 128
WIDTH = 512
PER_STEP = WIDTH // 512
GSIZE = 16
SUB = 8
RANKS = 8
F32, BF16 = jnp.float32, jnp.bfloat16

PARTS = (("y_hi", 2), ("x_hi", 2), ("x_lo", 2), ("z", 12), ("y_lo", 4), ("core", 2))
Y = ("y_hi", "y_lo", "core")
X = ("x_hi", "x_lo")
XZ = X + ("z",)
SHARE = ("x_lo",) + Y
ALL = tuple(name for name, _ in PARTS)
ZERO = ("z", "y_lo", "core")
N_Y = 16
N_Z = 12
N_YL = 4
N_X = 4


def iota(shape, dim):
    return lax.broadcasted_iota(jnp.int32, shape, dim)


def exchange(values, axes):
    return lax.all_to_all(values, axes, 0, 0, tiled=True)


def first_kernel(count_ref, plan_ref, filter_ref, out_ref, tile_ref):
    lane = iota((SUB, LANES), 1)
    row = iota((SUB, LANES), 0)
    tile_ref[...] = jnp.zeros((SUB, LANES), F32)
    tile_ref[0:SHORT, 0:64] = filter_ref[...].astype(F32)
    live = jnp.where(lane == plan_ref[0], count_ref[0].astype(F32), 0.0)
    tile = jnp.where(row == SHORT, live, tile_ref[...]).astype(BF16)
    for i in range(out_ref.shape[0]):
        out_ref[i] = tile


def pair_kernel(x_ref, got_ref, out_ref):
    lane = iota((SUB, LANES), 1)
    row = iota((SUB, LANES), 0)
    tiles = [got_ref[i].astype(F32) for i in range(N_Y)]
    live = tiles[0]
    for tile in tiles[1:]:
        live = live + tile
    high = jnp.floor(live * (1.0 / 64.0))
    low = pltpu.roll(live - 64.0 * high, SUB, 1)
    live = jnp.where(lane < SUB, high, jnp.where(lane < 2 * SUB, low, 0.0))
    out = jnp.zeros((SUB, LANES), F32)
    for yl in range(N_YL):
        both = jnp.where(lane < 64, tiles[2 * yl], pltpu.roll(tiles[2 * yl + 1], 64, 1))
        out = jnp.where(x_ref[0] == yl, both, out)
    out = jnp.where(row == SHORT, live, out).astype(BF16)
    for i in range(out_ref.shape[0]):
        out_ref[i] = out


def merge_kernel(got_ref, out_ref):
    total = got_ref[0].astype(F32)
    for i in range(1, N_Y):
        total = total + got_ref[i].astype(F32)
    for xl in range(2):
        medium = total[4 * N_Z + 4 * xl : 4 * N_Z + 4 * xl + 4]
        for z in range(N_Z):
            tile = jnp.concatenate([total[4 * z : 4 * z + 4], medium], 0).astype(BF16)
            for xh in range(N_X // 2):
                out_ref[(2 * xh + xl) * N_Z + z] = tile


def final_kernel(got_ref, short_ref, out_ref):
    total = got_ref[0].astype(F32)
    for i in range(1, got_ref.shape[0]):
        total = total + got_ref[i].astype(F32)
    short_ref[0:4, :] = total[0:4, :64]
    short_ref[4:SHORT, :] = total[0 : SHORT - 4, 64:]
    medium = total[4:]
    for i in range(out_ref.shape[0]):
        out_ref[i] = medium


def prepare_kernel(seg_ref, medium_ref, down_ref, up_ref, linked_ref, forward_ref, backward_ref, taps_ref, rtaps_ref):
    rows, cols = iota((TILE, TILE), 0), iota((TILE, TILE), 1)
    along = jnp.broadcast_to(seg_ref[...].astype(F32), (TILE, TILE))
    same = along == along.T
    lower, upper = same & (rows >= cols), same & (rows <= cols)

    @pl.when(pl.program_id(0) == 0)
    def _():
        for j in range(1, SHORT):
            down_ref[pl.ds((j - 1) * TILE, TILE), :] = jnp.where(same & (rows - cols == j), 1.0, 0.0).astype(BF16)
            up_ref[pl.ds((j - 1) * TILE, TILE), :] = jnp.where(same & (cols - rows == j), 1.0, 0.0).astype(BF16)
        flip = jnp.where(rows + cols == TILE - 1, 1.0, 0.0).astype(BF16)
        down_ref[pl.ds((SHORT - 1) * TILE, TILE), :] = flip
        linked_ref[...] = jnp.dot(flip, jnp.where(upper, 1.0, 0.0).astype(BF16), preferred_element_type=F32)
        taps = medium_ref[...].T.astype(BF16)
        taps_ref[...] = taps.astype(F32)
        rtaps_ref[...] = pltpu.roll(jnp.dot(taps, flip, preferred_element_type=F32), 1, 1)

    n = forward_ref.shape[1] // TILE
    at = pl.ds(pl.multiple_of(pl.program_id(0) * n, n), n)
    taps, rtaps = taps_ref[at, :], rtaps_ref[at, :]
    for g in range(n):
        where = slice(g * TILE, (g + 1) * TILE)
        base = jnp.broadcast_to(rtaps[g : g + 1, :], (TILE, TILE))
        base = pltpu.roll(base, 0, 1, stride=1, stride_axis=0)
        forward_ref[:, where] = jnp.where(lower, base, 0.0).astype(BF16)
        base = jnp.broadcast_to(taps[g : g + 1, :], (TILE, TILE))
        base = pltpu.roll(base, 0, 1, stride=1, stride_axis=0)
        backward_ref[:, where] = jnp.where(upper, base, 0.0).astype(BF16)


def taps_here(every_ref, part, step):
    tiles = []
    for h in range(WIDTH // LANES):
        z = part * (N_Z // 3) + step * PER_STEP + h // N_YL
        tiles.append(every_ref[(h % N_YL) * N_Z + z].astype(F32))
    return jnp.concatenate(tiles, 1)


def tile_kernel(
    count_ref, plan_ref, fq_ref, fk_ref, fv_ref, every_ref, down_ref, linked_ref, forward_ref, backward_ref, cot_ref,
    mixed_ref, gq_ref, gk_ref, gv_ref, msg_ref,
    scale_ref, short_ref, med_ref,
):
    rows = iota((TILE, TILE), 0)
    step, steps = pl.program_id(0), pl.num_programs(0)
    halves = WIDTH // LANES
    per_half = LANES // GSIZE

    @pl.when(step == 0)
    def _():
        live = every_ref[0].astype(F32)
        for i in range(1, every_ref.shape[0]):
            live = live + every_ref[i].astype(F32)
        row8, lane8 = iota((SUB, LANES), 0), iota((SUB, LANES), 1)
        high = jnp.where((row8 == SHORT) & (lane8 == plan_ref[0]), 64.0 * live, 0.0)
        low = jnp.where((row8 == SHORT) & (lane8 == plan_ref[0] + RANKS), live, 0.0)
        total = jnp.sum(jnp.sum(high + low, 0, keepdims=True), 1, keepdims=True)
        tiles = every_ref.shape[0] * N_Y
        weighting = (TILE * tiles / RANKS) / jnp.broadcast_to(total, (TILE, TILE))
        scale_ref[...] = jnp.where(rows < count_ref[0], weighting, 0.0)

    linked = linked_ref[...] > 0.5
    scale = jnp.concatenate([scale_ref[...]] * halves, 1)
    living = iota((TILE, WIDTH), 0) < count_ref[0]
    lane_group = iota((TILE, LANES), 1) // GSIZE

    def conv(part, f_ref):
        feats = f_ref[...]
        taps = taps_here(every_ref, part, step)
        shifted = jnp.dot(down_ref[: (SHORT - 1) * TILE], feats, preferred_element_type=F32)
        total = feats.astype(F32) * taps[0:1]
        for j in range(1, SHORT):
            total = total + shifted[(j - 1) * TILE : j * TILE] * taps[j : j + 1]
        return total, shifted

    query, q_shift = conv(0, fq_ref)
    key, k_shift = conv(1, fk_ref)
    value, v_shift = conv(2, fv_ref)
    product = (key * value).astype(BF16)
    flipped = jnp.dot(down_ref[(SHORT - 1) * TILE :], product, preferred_element_type=F32).astype(BF16)
    gout = cot_ref[...].astype(F32) * scale
    glong = (gout * query).astype(BF16)
    zero = jnp.zeros((TILE, LANES), BF16)

    longs, gprods = [], []
    for half in range(halves):
        lanes = slice(half * LANES, (half + 1) * LANES)
        blocks = slice(half * per_half * TILE, (half + 1) * per_half * TILE)
        prod_half, glong_half, flip_half = product[:, lanes], glong[:, lanes], flipped[:, lanes]
        prods, glongs, flips = [], [], []
        for g in range(per_half):
            prods.append(jnp.where(lane_group == g, prod_half, zero))
            glongs.append(jnp.where(lane_group == g, glong_half, zero))
            flips.append(jnp.where(lane_group == g, flip_half, zero))
        longs.append(jnp.dot(forward_ref[:, blocks], jnp.concatenate(prods, 0), preferred_element_type=F32))
        gprods.append(jnp.dot(backward_ref[:, blocks], jnp.concatenate(glongs, 0), preferred_element_type=F32))
        crossed = lax.dot_general(
            jnp.concatenate(flips, 0), glong_half, (((1,), (1,)), ((), ())), preferred_element_type=F32
        )
        sums = []
        for g in range(per_half):
            part = jnp.where(linked, crossed[g * TILE : (g + 1) * TILE], 0.0)
            part = pltpu.roll(part, 1, 1, stride=1, stride_axis=0)
            sums.append(jnp.sum(part, 0, keepdims=True))
        med_ref[halves * step + half] = jnp.concatenate(sums, 0)
    long_conv = jnp.concatenate(longs, 1)
    gprod = jnp.concatenate(gprods, 1)
    mixed_ref[...] = jnp.where(living, query * long_conv, 0.0).astype(BF16)

    row8, lane8 = iota((SUB, LANES), 0), iota((SUB, LANES), 1)
    keep = (row8 < 4) == (lane8 < 64)

    def taps_grad(part, grad, f_ref, shifted, g_ref):
        g_ref[...] = grad.astype(BF16)
        sums = [jnp.sum(grad * f_ref[...].astype(F32), 0, keepdims=True)]
        for j in range(1, SHORT):
            sums.append(jnp.sum(grad * shifted[(j - 1) * TILE : j * TILE], 0, keepdims=True))
        sums.append(jnp.zeros((1, WIDTH), F32))
        sums = jnp.concatenate(sums, 0)
        for h in range(halves):
            tile = sums[:, h * LANES : (h + 1) * LANES]
            other = pltpu.roll(pltpu.roll(tile, 64, 1), 4, 0)
            z = part * (N_Z // 3) + step * PER_STEP + h // N_YL
            short_ref[z * N_YL + h % N_YL] = jnp.where(keep, tile, other)

    taps_grad(0, gout * long_conv, fq_ref, q_shift, gq_ref)
    taps_grad(1, gprod * value, fk_ref, k_shift, gk_ref)
    taps_grad(2, gprod * key, fv_ref, v_shift, gv_ref)

    @pl.when(step == steps - 1)
    def _():
        medium = jnp.concatenate([med_ref[i] for i in range(med_ref.shape[0])], 0).T
        for yl in range(N_YL):
            for core in range(2):
                tiles = [short_ref[z * N_YL + yl][4 * core : 4 * core + 4] for z in range(N_Z)]
                for yh in range(2):
                    to = yh * 2 * N_YL + yl * 2 + core
                    pieces = [medium[64 * xl + 4 * to : 64 * xl + 4 * to + 4] for xl in range(2)]
                    msg_ref[to] = jnp.concatenate(tiles + pieces, 0).astype(BF16)


def spread_kernel(gq_ref, gk_ref, gv_ref, every_ref, up_ref, dfeats_ref, stage_ref, sems):
    step, steps = pl.program_id(0), pl.num_programs(0)
    width = gq_ref.shape[1]

    def store(part, at):
        where = pl.multiple_of((part * steps + at) * width, width)
        return pltpu.make_async_copy(
            stage_ref.at[lax.rem(at, 2), part], dfeats_ref.at[:, pl.ds(where, width)], sems.at[lax.rem(at, 2), part]
        )

    @pl.when(step >= 2)
    def _():
        for part in range(3):
            store(part, step - 2).wait()

    for part, g_ref in enumerate((gq_ref, gk_ref, gv_ref)):
        grad = g_ref[...]
        taps = taps_here(every_ref, part, step)
        shifted = jnp.dot(up_ref[...], grad, preferred_element_type=F32)
        total = grad.astype(F32) * taps[0:1]
        for j in range(1, SHORT):
            total = total + shifted[(j - 1) * TILE : j * TILE] * taps[j : j + 1]
        stage_ref[lax.rem(step, 2), part] = total.astype(BF16)
        store(part, step).start()

    @pl.when(step == steps - 1)
    def _():
        for at in (steps - 2, steps - 1):
            for part in range(3):
                store(part, at).wait()


def whole(shape):
    return pl.BlockSpec(shape, lambda *_: (0,) * len(shape))


def block(rows=TILE, part=0, steps=0):
    return pl.BlockSpec((rows, WIDTH), lambda i: (0, part * steps + i))


SMEM = pl.BlockSpec(memory_space=pltpu.SMEM)
VMEM = pl.BlockSpec(memory_space=pltpu.VMEM)


def prepare_call(doc_ids, medium):
    groups = medium.shape[1]
    n = 16
    rows = pl.BlockSpec((TILE, n * TILE), lambda i: (0, i))
    return pl.pallas_call(
        prepare_kernel,
        grid=(groups // n,),
        in_specs=[whole((1, TILE)), whole(medium.shape)],
        out_specs=[VMEM, whole(((SHORT - 1) * TILE, TILE)), VMEM, rows, rows],
        out_shape=[
            pltpu.VMEM((SHORT * TILE, TILE), BF16),
            jax.ShapeDtypeStruct(((SHORT - 1) * TILE, TILE), BF16),
            pltpu.VMEM((TILE, TILE), F32),
            jax.ShapeDtypeStruct((TILE, groups * TILE), BF16),
            jax.ShapeDtypeStruct((TILE, groups * TILE), BF16),
        ],
        scratch_shapes=[pltpu.VMEM((groups, TILE), F32), pltpu.VMEM((groups, TILE), F32)],
        name="prepare",
    )(doc_ids, medium)


def tile_call(count, plan, feats, filters, down, linked, forward, backward, cotangent):
    width = cotangent.shape[1]
    steps = width // WIDTH
    toeplitz = pl.BlockSpec((TILE, forward.shape[1] // steps), lambda i: (0, i))
    message = (N_Y, 4 * N_Z + SUB, LANES)
    vmem = pltpu.VMEM
    part = jax.ShapeDtypeStruct(cotangent.shape, BF16)
    return pl.pallas_call(
        tile_kernel,
        grid=(steps,),
        in_specs=[SMEM, SMEM]
        + [block(TILE, p, steps) for p in range(3)]
        + [VMEM, VMEM, VMEM, toeplitz, toeplitz, block()],
        out_specs=[block(), block(), block(), block(), VMEM],
        out_shape=[part, part, part, part, pltpu.VMEM(message, BF16)],
        scratch_shapes=[
            vmem((TILE, TILE), F32),
            vmem((N_Z * N_YL, SUB, LANES), F32),
            vmem((forward.shape[1] // TILE // SUB, SUB, TILE), F32),
        ],
        name="tile",
    )(count, plan, feats, feats, feats, filters, down, linked, forward, backward, cotangent)


def spread_call(grads, filters, up):
    width = grads[0].shape[1]
    steps = width // WIDTH
    return pl.pallas_call(
        spread_kernel,
        grid=(steps,),
        in_specs=[block()] * 3 + [VMEM, whole(up.shape)],
        out_specs=pl.BlockSpec(memory_space=pl.ANY),
        out_shape=jax.ShapeDtypeStruct((TILE, 3 * width), BF16),
        scratch_shapes=[pltpu.VMEM((2, 3, TILE, WIDTH), BF16), pltpu.SemaphoreType.DMA((2, 3))],
        name="spread",
    )(*grads, filters, up)


def small_call(kernel, outs, *operands, scratch=()):
    in_specs = [
        pl.BlockSpec(memory_space=pltpu.SMEM if x.dtype == jnp.int32 else pltpu.VMEM) for x in operands
    ]
    operands = [
        x if x.dtype == jnp.int32 else pltpu.with_memory_space_constraint(x, pltpu.VMEM) for x in operands
    ]
    return pl.pallas_call(
        kernel,
        in_specs=in_specs,
        out_specs=[pl.BlockSpec(memory_space=pltpu.VMEM)] * len(outs),
        out_shape=[pltpu.VMEM(*o) if keep else jax.ShapeDtypeStruct(*o) for keep, *o in outs],
        scratch_shapes=scratch,
    )(*operands)


def gather_filters(short_filter, counts, plan):
    n_xz = N_X * N_Z
    (send,) = small_call(
        first_kernel, [(False, (N_Y, SUB, LANES), BF16)], counts, plan, short_filter,
        scratch=[pltpu.VMEM((SUB, LANES), F32)],
    )
    got = exchange(send, Y)
    where = lax.axis_index(X).astype(jnp.int32).reshape(1)
    (send,) = small_call(pair_kernel, [(True, (n_xz, SUB, LANES), BF16)], where, got)
    return pltpu.with_memory_space_constraint(exchange(send, XZ), pltpu.VMEM)


def reduce_grads(message):
    n_xz = N_X * N_Z
    got = exchange(message, Y)
    (send,) = small_call(merge_kernel, [(True, (n_xz, SUB, LANES), BF16)], got)
    got = exchange(send, XZ)
    short_grad, send = small_call(final_kernel, [(False, (SHORT, 64), F32), (True, (2 * N_Y, 4, LANES), F32)], got)
    return short_grad, exchange(send, SHARE).reshape(TILE, LANES)


def shards(feats, short_filter, medium_filter, doc_ids, counts, plan, cotangent):
    down, up, linked, forward, backward = prepare_call(doc_ids, medium_filter)
    filters = gather_filters(short_filter, counts, plan)
    mixed, gq, gk, gv, message = tile_call(
        counts, plan, feats, filters, down, linked, forward, backward, cotangent
    )
    feats_grad = spread_call((gq, gk, gv), filters, up)
    short_grad, medium_grad = reduce_grads(message)
    return mixed, feats_grad, short_grad, medium_grad


def solution(mesh):
    parts = Mesh(mesh.devices.reshape([size for _, size in PARTS]), ALL)
    in_specs = (P(ALL, None), P(None, ZERO), P(), P(ALL, None), P(ALL), P(ALL), P(ALL, None))
    out_specs = (P(ALL, None), P(ALL, None), P(None, ZERO), P())
    return jax.shard_map(shards, mesh=parts, in_specs=in_specs, out_specs=out_specs, check_vma=False)
```
